32 devices in a mesh: fsdp: 2 (over x), replica: 16 (over z, y, core).
Axes of the slice: x: 2, y: 2, z: 4, core: 2. Of those that a mesh axis runs over, the one named last changes fastest.
Arguments:
- tokens: bfloat16 [16384, 576], P(('fsdp', 'replica')), may hold values from -6 to 6
- attn_gain: bfloat16 [576], P('fsdp'), may hold values from 0.5 to 1.5
- w_query: bfloat16 [576, 576], P('fsdp'), may hold values from -4.25 to 4.25
- w_key: bfloat16 [576, 192], P('fsdp'), may hold values from -0.25 to 0.25
- w_value: bfloat16 [576, 192], P('fsdp'), may hold values from -0.25 to 0.25
- w_out: bfloat16 [576, 576], P(None, 'fsdp'), may hold values from -0.5 to 0.5
- ffn_gain: bfloat16 [576], P('fsdp'), may hold values from 0.5 to 1.5
- w_gate: bfloat16 [576, 1536], P('fsdp'), may hold values from -0.25 to 0.25
- w_up: bfloat16 [576, 1536], P('fsdp'), may hold values from -0.25 to 0.25
- w_down: bfloat16 [1536, 576], P(None, 'fsdp'), may hold values from -0.15625 to 0.15625
- cotangent: bfloat16 [16384, 576], P(('fsdp', 'replica')), may hold values from -6 to 6
Outputs:
- layer_out: bfloat16 [16384, 576], P(('fsdp', 'replica'))
- grad_tokens: float32 [16384, 576], P(('fsdp', 'replica'))
- grad_attn_gain: float32 [576], P('fsdp')
- grad_query: float32 [576, 576], P('fsdp')
- grad_key: float32 [576, 192], P('fsdp')
- grad_value: float32 [576, 192], P('fsdp')
- grad_out: float32 [576, 576], P(None, 'fsdp')
- grad_ffn_gain: float32 [576], P('fsdp')
- grad_gate: float32 [576, 1536], P('fsdp')
- grad_up: float32 [576, 1536], P('fsdp')
- grad_down: float32 [1536, 576], P(None, 'fsdp')
The draws below stay inside these ranges and needn't reach their ends.
All inputs are finite; a program needn't handle non-finite values.
Results may differ from the reference program's by a relative error of at most 0.022.
Values may be sent and summed in bfloat16 or wider, within the bound.
A program may use at most 128 MiB of HBM per device.

```python
import math
import jax
import jax.numpy as jnp
from jax import lax

D = 576
H = 9
KV = 3
HD = 64
FF = 1536
LEN = 256
SEQS = 64
TOKENS = 16384


KEY_LIMIT = 0.25


def paired(key):
    key_part = jax.random.truncated_normal(jax.random.fold_in(key, 11), -6.0, 6.0, (D, KV * HD), jnp.float32) * D ** (-0.5)
    noise_part = jax.random.truncated_normal(jax.random.fold_in(key, 12), -6.0, 6.0, (D, H * HD), jnp.float32) * D ** (-0.5)
    key_part = jnp.clip(key_part, -KEY_LIMIT, KEY_LIMIT)
    noise_part = jnp.clip(noise_part, -KEY_LIMIT, KEY_LIMIT)
    return (key_part, noise_part)


def draw_w_key(key, part):
    key_part, noise_part = paired(key)
    return key_part.astype(jnp.bfloat16)


def draw_w_query(key, part):
    key_part, noise_part = paired(key)
    return noise_part.astype(jnp.bfloat16)


def levels(key, shape, pieces, smallest, high):
    level, own = 1.0, jax.random.fold_in(key, 6)
    for dim, parts in pieces:
        steps = jnp.exp(jax.random.uniform(jax.random.fold_in(own, dim), (parts,), jnp.float32, smallest / len(pieces), high / len(pieces)))
        level = level * jnp.repeat(steps, shape[dim] // parts).reshape([-1 if axis == dim else 1 for axis in range(len(shape))])
    return level


def noise(own_key, extent, deviation, most, split=(), held_as=jnp.bfloat16):
    entries = deviation * jax.random.normal(own_key, extent, jnp.float32)
    if split:
        entries = entries * levels(own_key, extent, split, -0.22, 0.18)
    return jnp.clip(entries, -most, most).astype(held_as)


def setup_inputs(seed: int = 0) -> dict:
    arg_keys = jax.random.split(jax.random.key(seed), 12)
    tokens = noise(arg_keys[0], (TOKENS, D), 1.0, 6.0, ((0, 32),))
    attn_gain = jnp.clip(1.0 + 0.1 * jax.random.normal(arg_keys[1], (D,), jnp.float32), 0.5, 1.5).astype(jnp.bfloat16)
    w_query = draw_w_query(jax.random.fold_in(arg_keys[11], 71), 0)
    w_key = draw_w_key(jax.random.fold_in(arg_keys[11], 71), 0)
    w_value = noise(arg_keys[4], (D, KV * HD), D ** -0.5, 0.25, ((0, 2),))
    w_out = noise(arg_keys[5], (H * HD, D), (H * HD // 4) ** -0.5, 0.5, ((1, 2),))
    ffn_gain = jnp.clip(1.0 + 0.1 * jax.random.normal(arg_keys[6], (D,), jnp.float32), 0.5, 1.5).astype(jnp.bfloat16)
    w_gate = noise(arg_keys[7], (D, FF), D ** -0.5, 0.25, ((0, 2),))
    w_up = noise(arg_keys[8], (D, FF), D ** -0.5, 0.25, ((0, 2),))
    w_down = noise(arg_keys[9], (FF, D), FF ** -0.5, 0.15625, ((1, 2),))
    cotangent = noise(arg_keys[10], (TOKENS, D), 1.0, 6.0, ((0, 32),))
    return {"tokens": tokens, "attn_gain": attn_gain, "w_query": w_query, "w_key": w_key, "w_value": w_value, "w_out": w_out, "ffn_gain": ffn_gain, "w_gate": w_gate, "w_up": w_up, "w_down": w_down, "cotangent": cotangent}


NORM_EPS = 1e-05
ROPE_BASE = 100000.0
MASK_FILL = -1e+30

def tables(length, head_size):
    half_size = head_size // 2
    inv_freq = ROPE_BASE ** (-2.0 * jnp.arange(half_size, dtype=jnp.float32) / head_size)
    angles = jnp.arange(length, dtype=jnp.float32)[:, None] * inv_freq[None, :]
    return (jnp.cos(angles)[:, None, :], jnp.sin(angles)[:, None, :])

def rotate(values, cosine, sine_tab, direction):
    half_size = values.shape[-1] // 2
    lower_half = values[..., :half_size]
    upper_half = values[..., half_size:]
    return jnp.concatenate([lower_half * cosine - direction * upper_half * sine_tab, upper_half * cosine + direction * lower_half * sine_tab], axis=-1)

def norm_rows(values, gain_vec):
    inv_rms = lax.rsqrt(lax.optimization_barrier(jnp.mean(values * values, axis=-1, keepdims=True)) + NORM_EPS)
    return (values * inv_rms * gain_vec, inv_rms)

def norm_back(values, inv_rms, gain_vec, grad_in):
    normed = values * inv_rms
    d_normed = grad_in * gain_vec
    d_values = inv_rms * (d_normed - normed * lax.optimization_barrier(jnp.mean(d_normed * normed, axis=-1, keepdims=True)))
    return (d_values, lax.optimization_barrier(jnp.sum(grad_in * normed, axis=0)))

def as_f32(array):
    return array.astype(jnp.float32)

def block_pass(tokens, cotangent, attn_gain, w_query, w_key, w_value, w_out, ffn_gain, w_gate, w_up, w_down):
    row_count = tokens.shape[0]
    seq_count = row_count // LEN
    groups = H // KV
    cosine, sine_tab = tables(LEN, HD)
    tokens_f = as_f32(tokens)
    gain_one = as_f32(attn_gain)
    normed_f, inv_rms1 = norm_rows(tokens_f, gain_one)
    normed1 = normed_f.astype(jnp.bfloat16)
    query_pre = jnp.dot(normed1, w_query, preferred_element_type=jnp.float32).reshape(seq_count, LEN, H, HD)
    query_rot = rotate(query_pre, cosine, sine_tab, 1.0).astype(jnp.bfloat16).reshape(seq_count, LEN, KV, groups, HD)
    key_pre = jnp.dot(normed1, w_key, preferred_element_type=jnp.float32).reshape(seq_count, LEN, KV, HD)
    key_rot = rotate(key_pre, cosine, sine_tab, 1.0).astype(jnp.bfloat16)
    values = jnp.dot(normed1, w_value, preferred_element_type=jnp.float32).reshape(seq_count, LEN, KV, HD).astype(jnp.bfloat16)
    scores = jnp.einsum('sikgd,sjkd->skgij', as_f32(query_rot), as_f32(key_rot)) * HD ** (-0.5)
    causal = jnp.arange(LEN)[:, None] >= jnp.arange(LEN)[None, :]
    scores = jnp.where(causal, scores, MASK_FILL)
    row_max = lax.optimization_barrier(jnp.max(scores, axis=-1, keepdims=True))
    log_total = row_max + jnp.log(lax.optimization_barrier(jnp.sum(jnp.exp(scores - row_max), axis=-1, keepdims=True)))
    prob_f = jnp.exp(scores - log_total)
    attn_prob = prob_f.astype(jnp.bfloat16)
    context = jnp.einsum('skgij,sjkd->sikgd', as_f32(attn_prob), as_f32(values)).astype(jnp.bfloat16).reshape(row_count, H * HD)
    mid_sum = tokens_f + jnp.dot(context, w_out, preferred_element_type=jnp.float32)
    gain_two = as_f32(ffn_gain)
    normed_g, inv_rms2 = norm_rows(mid_sum, gain_two)
    normed2 = normed_g.astype(jnp.bfloat16)
    gate_pre = jnp.dot(normed2, w_gate, preferred_element_type=jnp.float32)
    up_proj = jnp.dot(normed2, w_up, preferred_element_type=jnp.float32)
    sigmoid_g = jax.nn.sigmoid(gate_pre)
    act_gate = gate_pre * sigmoid_g
    hidden = (act_gate * up_proj).astype(jnp.bfloat16)
    layer_out = (mid_sum + jnp.dot(hidden, w_down, preferred_element_type=jnp.float32)).astype(jnp.bfloat16)
    grad_down = jnp.dot(hidden.T, cotangent, preferred_element_type=jnp.float32)
    d_hidden = jnp.dot(cotangent, w_down.T, preferred_element_type=jnp.float32)
    d_up = (d_hidden * act_gate).astype(jnp.bfloat16)
    d_gate = (d_hidden * up_proj * sigmoid_g * (1.0 + gate_pre * (1.0 - sigmoid_g))).astype(jnp.bfloat16)
    grad_gate = jnp.dot(normed2.T, d_gate, preferred_element_type=jnp.float32)
    grad_up = jnp.dot(normed2.T, d_up, preferred_element_type=jnp.float32)
    d_normed2 = jnp.dot(d_gate, w_gate.T, preferred_element_type=jnp.float32) + jnp.dot(d_up, w_up.T, preferred_element_type=jnp.float32)
    d_mid_n, grad_ffn_gain = norm_back(mid_sum, inv_rms2, gain_two, d_normed2)
    d_mid = as_f32(cotangent) + d_mid_n
    d_mid_b = d_mid.astype(jnp.bfloat16)
    grad_out = jnp.dot(context.T, d_mid_b, preferred_element_type=jnp.float32)
    d_context = jnp.dot(d_mid_b, w_out.T, preferred_element_type=jnp.float32).astype(jnp.bfloat16).reshape(seq_count, LEN, KV, groups, HD)
    d_values = jnp.einsum('skgij,sikgd->sjkd', as_f32(attn_prob), as_f32(d_context))
    d_prob = jnp.einsum('sikgd,sjkd->skgij', as_f32(d_context), as_f32(values))
    row_delta = lax.optimization_barrier(jnp.sum(prob_f * d_prob, axis=-1, keepdims=True))
    d_scores = (prob_f * (d_prob - row_delta) * HD ** (-0.5)).astype(jnp.bfloat16)
    d_query = jnp.einsum('skgij,sjkd->sikgd', as_f32(d_scores), as_f32(key_rot)).reshape(seq_count, LEN, H, HD)
    d_key = jnp.einsum('skgij,sikgd->sjkd', as_f32(d_scores), as_f32(query_rot))
    d_query_b = rotate(d_query, cosine, sine_tab, -1.0).astype(jnp.bfloat16).reshape(row_count, H * HD)
    d_key_b = rotate(d_key, cosine, sine_tab, -1.0).astype(jnp.bfloat16).reshape(row_count, KV * HD)
    d_values_b = d_values.astype(jnp.bfloat16).reshape(row_count, KV * HD)
    grad_query = jnp.dot(normed1.T, d_query_b, preferred_element_type=jnp.float32)
    grad_key = jnp.dot(normed1.T, d_key_b, preferred_element_type=jnp.float32)
    grad_value = jnp.dot(normed1.T, d_values_b, preferred_element_type=jnp.float32)
    d_normed1 = jnp.dot(d_query_b, w_query.T, preferred_element_type=jnp.float32) + jnp.dot(d_key_b, w_key.T, preferred_element_type=jnp.float32) + jnp.dot(d_values_b, w_value.T, preferred_element_type=jnp.float32)
    d_tok_n, grad_attn_gain = norm_back(tokens_f, inv_rms1, gain_one, d_normed1)
    grad_tokens = d_mid + d_tok_n
    return (layer_out, grad_tokens, (grad_attn_gain, grad_query, grad_key, grad_value, grad_out, grad_ffn_gain, grad_gate, grad_up, grad_down))

def reference(tokens, attn_gain, w_query, w_key, w_value, w_out, ffn_gain, w_gate, w_up, w_down, cotangent):
    block_seqs = math.gcd(SEQS, max(1, 4096 // LEN))
    block_count = SEQS // block_seqs
    block_rows = block_seqs * LEN
    weight_list = (attn_gain, w_query, w_key, w_value, w_out, ffn_gain, w_gate, w_up, w_down)
    zero_grads = tuple((jnp.zeros(weight.shape, jnp.float32) for weight in weight_list))
    inputs = (tokens.reshape(block_count, block_rows, D), cotangent.reshape(block_count, block_rows, D))

    def scan_step(totals, block_pair):
        block_out, block_grad, block_terms = block_pass(block_pair[0], block_pair[1], attn_gain, w_query, w_key, w_value, w_out, ffn_gain, w_gate, w_up, w_down)
        return (jax.tree.map(jnp.add, totals, block_terms), (block_out, block_grad))
    totals, (outs_all, grads_all) = lax.scan(scan_step, zero_grads, inputs)
    return (outs_all.reshape(TOKENS, D), grads_all.reshape(TOKENS, D), totals[0], totals[1], totals[2], totals[3], totals[4], totals[5], totals[6], totals[7], totals[8])
```

```python
import functools

import jax
import jax.numpy as jnp
from jax import lax
from jax.sharding import PartitionSpec as P

H = 9
KV = 3
HD = 64
LEN = 256


NORM_EPS = 1e-05
ROPE_BASE = 100000.0
MASK_FILL = -1e30


def tables(length, head_size):
    half_size = head_size // 2
    inv_freq = ROPE_BASE ** (-2.0 * jnp.arange(half_size, dtype=jnp.float32) / head_size)
    angles = jnp.arange(length, dtype=jnp.float32)[:, None] * inv_freq[None, :]
    return (jnp.cos(angles)[:, None, :], jnp.sin(angles)[:, None, :])


def rotate(values, cosine, sine_tab, direction):
    half_size = values.shape[-1] // 2
    lower_half = values[..., :half_size]
    upper_half = values[..., half_size:]
    return jnp.concatenate(
        [
            lower_half * cosine - direction * upper_half * sine_tab,
            upper_half * cosine + direction * lower_half * sine_tab,
        ],
        axis=-1,
    )


def norm_rows(values, gain_vec):
    inv_rms = lax.rsqrt(jnp.mean(values * values, axis=-1, keepdims=True) + NORM_EPS)
    return (values * inv_rms * gain_vec, inv_rms)


def norm_back(values, inv_rms, gain_vec, grad_in):
    normed = values * inv_rms
    d_normed = grad_in * gain_vec
    d_values = inv_rms * (d_normed - normed * jnp.mean(d_normed * normed, axis=-1, keepdims=True))
    return (d_values, jnp.sum(grad_in * normed, axis=0))


def dot_right_t(left_op, right_op):
    return lax.dot_general(
        left_op, right_op, (((1,), (1,)), ((), ())), preferred_element_type=jnp.float32
    )


def dot_left_t(left_op, right_op):
    return lax.dot_general(
        left_op, right_op, (((0,), (0,)), ((), ())), preferred_element_type=jnp.float32
    )


def causal_scores(query_rot, key_rot):
    length = query_rot.shape[1]
    scores = jnp.einsum(
        "sikgd,sjkd->skgij", query_rot, key_rot, preferred_element_type=jnp.float32
    ) * HD ** (-0.5)
    causal = jnp.arange(length)[:, None] >= jnp.arange(length)[None, :]
    return jnp.where(causal, scores, MASK_FILL)


def attn_forward(tokens, weight_set):
    w_query, w_key, w_value, w_out, gain_vec = weight_set
    row_count = tokens.shape[0]
    seq_count = row_count // LEN
    groups = H // KV
    cosine, sine_tab = tables(LEN, HD)
    tokens_f = tokens.astype(jnp.float32)
    gain_one = gain_vec.astype(jnp.float32)
    normed_f, inv_rms1 = norm_rows(tokens_f, gain_one)
    normed1 = normed_f.astype(jnp.bfloat16)
    query_pre = jnp.dot(normed1, w_query, preferred_element_type=jnp.float32).reshape(
        seq_count, LEN, H, HD
    )
    query_rot = (
        rotate(query_pre, cosine, sine_tab, 1.0)
        .astype(jnp.bfloat16)
        .reshape(seq_count, LEN, KV, groups, HD)
    )
    key_pre = jnp.dot(normed1, w_key, preferred_element_type=jnp.float32).reshape(
        seq_count, LEN, KV, HD
    )
    key_rot = rotate(key_pre, cosine, sine_tab, 1.0).astype(jnp.bfloat16)
    values = (
        jnp.dot(normed1, w_value, preferred_element_type=jnp.float32)
        .reshape(seq_count, LEN, KV, HD)
        .astype(jnp.bfloat16)
    )
    scores = causal_scores(query_rot, key_rot)
    row_max = jnp.max(scores, axis=-1, keepdims=True)
    log_total = row_max + jnp.log(jnp.sum(jnp.exp(scores - row_max), axis=-1, keepdims=True))
    attn_prob = jnp.exp(scores - log_total).astype(jnp.bfloat16)
    context = (
        jnp.einsum("skgij,sjkd->sikgd", attn_prob, values, preferred_element_type=jnp.float32)
        .astype(jnp.bfloat16)
        .reshape(row_count, H * HD)
    )
    mid_sum = tokens_f + dot_right_t(context, w_out)
    return (
        mid_sum,
        (tokens_f, inv_rms1, gain_one, normed1, query_rot, key_rot, values, log_total, context),
    )


def ffn_forward(mid_sum, weight_set):
    w_gate, w_up, w_down, gain_vec = weight_set
    gain_two = gain_vec.astype(jnp.float32)
    normed_g, inv_rms2 = norm_rows(mid_sum, gain_two)
    normed2 = normed_g.astype(jnp.bfloat16)
    gate_pre = jnp.dot(normed2, w_gate, preferred_element_type=jnp.float32)
    up_proj = jnp.dot(normed2, w_up, preferred_element_type=jnp.float32)
    sigmoid_g = jax.nn.sigmoid(gate_pre)
    act_gate = gate_pre * sigmoid_g
    hidden = (act_gate * up_proj).astype(jnp.bfloat16)
    layer_out = (mid_sum + dot_right_t(hidden, w_down)).astype(
        jnp.bfloat16
    )
    return (
        layer_out,
        (inv_rms2, gain_two, normed2, gate_pre, up_proj, sigmoid_g, act_gate, hidden),
    )


def ffn_backward(cotangent, mid_sum, kept, weight_set):
    w_gate, w_up, w_down, gain_vec = weight_set
    inv_rms2, gain_two, normed2, gate_pre, up_proj, sigmoid_g, act_gate, hidden = kept
    d_hidden = jnp.dot(cotangent, w_down, preferred_element_type=jnp.float32)
    d_up = (d_hidden * act_gate).astype(jnp.bfloat16)
    d_gate = (d_hidden * up_proj * sigmoid_g * (1.0 + gate_pre * (1.0 - sigmoid_g))).astype(
        jnp.bfloat16
    )
    d_normed2 = dot_right_t(d_gate, w_gate) + dot_right_t(d_up, w_up)
    d_mid_n, term_gain = norm_back(mid_sum, inv_rms2, gain_two, d_normed2)
    d_mid = cotangent.astype(jnp.float32) + d_mid_n
    return (d_mid, (d_gate, d_up, term_gain))


def attn_backward(d_mid, kept, weight_set):
    w_query, w_key, w_value, w_out, gain_vec = weight_set
    tokens_f, inv_rms1, gain_one, normed1, query_rot, key_rot, values, log_total, context = kept
    row_count = tokens_f.shape[0]
    seq_count = row_count // LEN
    groups = H // KV
    cosine, sine_tab = tables(LEN, HD)
    d_mid_b = d_mid.astype(jnp.bfloat16)
    term_out = dot_left_t(d_mid_b, context)
    d_context = (
        jnp.dot(d_mid_b, w_out, preferred_element_type=jnp.float32).astype(jnp.bfloat16).reshape(seq_count, LEN, KV, groups, HD)
    )
    prob_f = jnp.exp(causal_scores(query_rot, key_rot) - log_total)
    attn_prob = prob_f.astype(jnp.bfloat16)
    d_values = jnp.einsum(
        "skgij,sikgd->sjkd", attn_prob, d_context, preferred_element_type=jnp.float32
    )
    d_prob = jnp.einsum("sikgd,sjkd->skgij", d_context, values, preferred_element_type=jnp.float32)
    row_delta = jnp.sum(prob_f * d_prob, axis=-1, keepdims=True)
    d_scores = (prob_f * (d_prob - row_delta) * HD ** (-0.5)).astype(jnp.bfloat16)
    d_query = jnp.einsum(
        "skgij,sjkd->sikgd", d_scores, key_rot, preferred_element_type=jnp.float32
    ).reshape(seq_count, LEN, H, HD)
    d_key = jnp.einsum("skgij,sikgd->sjkd", d_scores, query_rot, preferred_element_type=jnp.float32)
    d_query_b = (
        rotate(d_query, cosine, sine_tab, -1.0).astype(jnp.bfloat16).reshape(row_count, H * HD)
    )
    d_key_b = rotate(d_key, cosine, sine_tab, -1.0).astype(jnp.bfloat16).reshape(row_count, KV * HD)
    d_values_b = d_values.astype(jnp.bfloat16).reshape(row_count, KV * HD)
    term_query = dot_left_t(normed1, d_query_b)
    term_key = dot_left_t(normed1, d_key_b)
    term_value = dot_left_t(normed1, d_values_b)
    d_normed1 = (
        dot_right_t(d_query_b, w_query)
        + dot_right_t(d_key_b, w_key)
        + dot_right_t(d_values_b, w_value)
    )
    d_tok_n, term_gain = norm_back(tokens_f, inv_rms1, gain_one, d_normed1)
    grad_tokens = d_mid + d_tok_n
    return (grad_tokens, (term_gain, term_query, term_key, term_value, term_out))


AXES = ("fsdp", "replica")


def bits_of(count):
    return count.bit_length() - 1


class Plan:
    def __init__(self, groups, copies):
        self.groups, self.copies = groups, copies
        self.group_bits, self.copy_bits = bits_of(groups), bits_of(copies)

    def swap(self, array, partner):
        pairs = []
        for group in range(self.groups):
            for copy in range(self.copies):
                to_group, to_copy = partner(group, copy)
                pairs.append((group * self.copies + copy, to_group * self.copies + to_copy))
        return lax.ppermute(array, AXES, pairs)

    def swap_group(self, array, bit):
        return self.swap(array, lambda g, r: (g ^ (1 << bit), r))

    def swap_copy(self, array, bit):
        return self.swap(array, lambda g, r: (g, r ^ (1 << bit)))

    def where(self):
        return lax.axis_index("fsdp"), lax.axis_index("replica")


def bit_at(index, bit):
    return lax.rem(lax.div(index, 1 << bit), 2)


def joined(mine, theirs, bit, axis):
    return jnp.where(
        bit == 0,
        jnp.concatenate([mine, theirs], axis=axis),
        jnp.concatenate([theirs, mine], axis=axis),
    )


def whole_rows(plan, shard):
    group, copy = plan.where()
    half = shard.shape[0] // 2
    core = bit_at(copy, 0)
    held = lax.dynamic_slice_in_dim(shard, core * half, half, axis=0)[None, None]
    for bit in range(plan.group_bits):
        held = joined(held, plan.swap_group(held, bit), bit_at(group, bit), 0)
    held = joined(held, plan.swap_copy(held, 0), core, 1)
    return held.reshape(plan.groups * shard.shape[0], shard.shape[1])


def whole_gains(plan, gains):
    group, _ = plan.where()
    held = gains
    for bit in range(plan.group_bits):
        held = joined(held, plan.swap_group(held, bit), bit_at(group, bit), 1)
    return held


def added(left, right):
    return (left.astype(jnp.float32) + right.astype(jnp.float32)).astype(jnp.bfloat16)


def pick(array, bit, axis=0):
    size = array.shape[axis] // 2
    mine = lax.dynamic_slice_in_dim(array, bit * size, size, axis=axis)
    theirs = lax.dynamic_slice_in_dim(array, (1 - bit) * size, size, axis=axis)
    return mine, theirs


def summed_rows(plan, term):
    group, copy = plan.where()
    core = bit_at(copy, 0)
    rows, columns = term.shape[0] // plan.groups, term.shape[1]
    quarter = columns // 4
    term = term.astype(jnp.bfloat16)
    blocks = term.reshape(plan.groups, rows, 2, 2, quarter).transpose(2, 3, 0, 1, 4)
    mine, theirs = pick(blocks, core)
    held = added(mine, plan.swap_copy(theirs, 0))[0]
    steps = plan.group_bits
    held = held.reshape((2,) * (steps + 1) + (rows, quarter))
    held = jnp.where(core == 0, jnp.moveaxis(held, 0, steps), held)
    for step in range(steps + 1):
        group_bit = [steps - 1 - step, steps - step]
        first = bit_at(group, group_bit[0]) if step < steps else bit_at(copy, 1)
        second = bit_at(group, group_bit[1]) if step > 0 else bit_at(copy, 1)
        mine, theirs = pick(held, jnp.where(core == 0, first, second))

        def partner(g, r):
            order = r % 2
            if (order == 0 and step == steps) or (order == 1 and step == 0):
                return g, r ^ 2
            return g ^ (1 << group_bit[order]), r

        held = added(mine, plan.swap(theirs, partner))[0]
    for bit in range(2, plan.copy_bits):
        mine, theirs = pick(held, bit_at(copy, bit))
        held = added(mine, plan.swap_copy(theirs, bit))
    for bit in range(plan.copy_bits - 1, 1, -1):
        held = joined(held, plan.swap_copy(held, bit), bit_at(copy, bit), 0)
    held = joined(held, plan.swap_copy(held, 1), bit_at(copy, 1), 1)
    held = joined(held, plan.swap_copy(held, 0), core, 1)
    return held.astype(jnp.float32)


def summed_gains(plan, gains):
    group, _ = plan.where()
    held = gains
    for bit in range(plan.copy_bits):
        held = held + plan.swap_copy(held, bit)
    for bit in range(plan.group_bits):
        held = held + plan.swap_group(held, bit)
    size = gains.shape[1] // plan.groups
    return lax.dynamic_slice_in_dim(held, group * size, size, axis=1)


def on_device(
    plan,
    tokens,
    attn_gain,
    w_query,
    w_key,
    w_value,
    w_out,
    ffn_gain,
    w_gate,
    w_up,
    w_down,
    cotangent,
):
    gains = whole_gains(plan, jnp.stack([attn_gain, ffn_gain]))
    qkv = whole_rows(plan, jnp.concatenate([w_query, w_key, w_value], axis=1))
    q_size, k_size = w_query.shape[1], w_key.shape[1]
    full_query, full_key, full_value = (
        qkv[:, :q_size],
        qkv[:, q_size : q_size + k_size],
        qkv[:, q_size + k_size :],
    )
    full_out = whole_rows(plan, w_out.T)
    full_gate = whole_rows(plan, w_gate)
    full_up = whole_rows(plan, w_up)
    full_down = whole_rows(plan, w_down.T)
    attn_set = (full_query, full_key, full_value, full_out, gains[0])
    ffn_set = (full_gate, full_up, full_down, gains[1])
    mid_sum, attn_kept = attn_forward(tokens, attn_set)
    layer_out, ffn_kept = ffn_forward(mid_sum, ffn_set)
    d_mid, ffn_parts = ffn_backward(cotangent, mid_sum, ffn_kept, ffn_set)
    d_gate, d_up, term_gain2 = ffn_parts
    normed2 = ffn_kept[2]
    hidden = ffn_kept[7]
    term_gate = dot_left_t(normed2, d_gate)
    term_up = dot_left_t(normed2, d_up)
    term_down = dot_left_t(cotangent, hidden)
    ffn_terms = jnp.concatenate(
        [term.astype(jnp.bfloat16) for term in (term_gate, term_up, term_down)], axis=1
    )
    ffn_grads = summed_rows(plan, ffn_terms)
    inner = term_gate.shape[1]
    grad_gate = ffn_grads[:, :inner]
    grad_up = ffn_grads[:, inner : 2 * inner]
    grad_down = ffn_grads[:, 2 * inner :].T
    grad_tokens, attn_terms = attn_backward(d_mid, attn_kept, attn_set)
    term_gain1, term_query, term_key, term_value, term_out = attn_terms
    gain_grads = summed_gains(plan, jnp.stack([term_gain1, term_gain2]))
    attn_cat = jnp.concatenate(
        [term.astype(jnp.bfloat16) for term in (term_query, term_key, term_value, term_out)],
        axis=1,
    )
    attn_grads = summed_rows(plan, attn_cat)
    v_end = q_size + 2 * k_size
    return (
        layer_out,
        grad_tokens,
        gain_grads[0],
        attn_grads[:, :q_size],
        attn_grads[:, q_size : q_size + k_size],
        attn_grads[:, q_size + k_size : v_end],
        attn_grads[:, v_end:].T,
        gain_grads[1],
        grad_gate,
        grad_up,
        grad_down,
    )


def solution(mesh):
    plan = Plan(mesh.shape["fsdp"], mesh.shape["replica"])
    return jax.shard_map(
        functools.partial(on_device, plan),
        mesh=mesh,
        in_specs=(
            P(("fsdp", "replica"), None),
            P("fsdp"),
            P("fsdp", None),
            P("fsdp", None),
            P("fsdp", None),
            P(None, "fsdp"),
            P("fsdp"),
            P("fsdp", None),
            P("fsdp", None),
            P(None, "fsdp"),
            P(("fsdp", "replica"), None),
        ),
        out_specs=(
            P(("fsdp", "replica"), None),
            P(("fsdp", "replica"), None),
            P("fsdp"),
            P("fsdp", None),
            P("fsdp", None),
            P("fsdp", None),
            P(None, "fsdp"),
            P("fsdp"),
            P("fsdp", None),
            P("fsdp", None),
            P(None, "fsdp"),
        ),
        check_vma=False,
    )
```

```python
import functools

import jax
import jax.numpy as jnp
from jax import lax
from jax.sharding import PartitionSpec as P

H = 9
KV = 3
HD = 64
LEN = 256


NORM_EPS = 1e-05
ROPE_BASE = 100000.0
MASK_FILL = -1e30


def tables(length, head_size):
    half_size = head_size // 2
    inv_freq = ROPE_BASE ** (-2.0 * jnp.arange(half_size, dtype=jnp.float32) / head_size)
    angles = jnp.arange(length, dtype=jnp.float32)[:, None] * inv_freq[None, :]
    return (jnp.cos(angles)[:, None, :], jnp.sin(angles)[:, None, :])


def rotate(values, cosine, sine_tab, direction):
    half_size = values.shape[-1] // 2
    lower_half = values[..., :half_size]
    upper_half = values[..., half_size:]
    return jnp.concatenate(
        [
            lower_half * cosine - direction * upper_half * sine_tab,
            upper_half * cosine + direction * lower_half * sine_tab,
        ],
        axis=-1,
    )


def norm_rows(values, gain_vec):
    inv_rms = lax.rsqrt(jnp.mean(values * values, axis=-1, keepdims=True) + NORM_EPS)
    return (values * inv_rms * gain_vec, inv_rms)


def norm_back(values, inv_rms, gain_vec, grad_in):
    normed = values * inv_rms
    d_normed = grad_in * gain_vec
    d_values = inv_rms * (d_normed - normed * jnp.mean(d_normed * normed, axis=-1, keepdims=True))
    return (d_values, jnp.sum(grad_in * normed, axis=0))


def dot_right_t(left_op, right_op):
    return lax.dot_general(
        left_op, right_op, (((1,), (1,)), ((), ())), preferred_element_type=jnp.float32
    )


def dot_left_t(left_op, right_op):
    return lax.dot_general(
        left_op, right_op, (((0,), (0,)), ((), ())), preferred_element_type=jnp.float32
    )


def causal_scores(query_rot, key_rot):
    length = query_rot.shape[1]
    scores = jnp.einsum(
        "sikgd,sjkd->skgij", query_rot, key_rot, preferred_element_type=jnp.float32
    ) * HD ** (-0.5)
    causal = jnp.arange(length)[:, None] >= jnp.arange(length)[None, :]
    return jnp.where(causal, scores, MASK_FILL)


def attn_forward(tokens, weight_set, waiting):
    w_query, w_key, w_value, w_out, gain_vec = weight_set
    row_count = tokens.shape[0]
    seq_count = row_count // LEN
    groups = H // KV
    cosine, sine_tab = tables(LEN, HD)
    tokens_f = tokens.astype(jnp.float32)
    gain_one = gain_vec.astype(jnp.float32)
    normed_f, inv_rms1 = norm_rows(tokens_f, gain_one)
    normed1 = normed_f.astype(jnp.bfloat16)
    query_pre = jnp.dot(normed1, w_query, preferred_element_type=jnp.float32).reshape(
        seq_count, LEN, H, HD
    )
    query_rot = (
        rotate(query_pre, cosine, sine_tab, 1.0)
        .astype(jnp.bfloat16)
        .reshape(seq_count, LEN, KV, groups, HD)
    )
    key_pre = jnp.dot(normed1, w_key, preferred_element_type=jnp.float32).reshape(
        seq_count, LEN, KV, HD
    )
    key_rot = rotate(key_pre, cosine, sine_tab, 1.0).astype(jnp.bfloat16)
    values = (
        jnp.dot(normed1, w_value, preferred_element_type=jnp.float32)
        .reshape(seq_count, LEN, KV, HD)
        .astype(jnp.bfloat16)
    )
    scores = causal_scores(query_rot, key_rot)
    scores, waiting = tied(scores, waiting)
    row_max = jnp.max(scores, axis=-1, keepdims=True)
    log_total = row_max + jnp.log(jnp.sum(jnp.exp(scores - row_max), axis=-1, keepdims=True))
    attn_prob = jnp.exp(scores - log_total).astype(jnp.bfloat16)
    context = (
        jnp.einsum("skgij,sjkd->sikgd", attn_prob, values, preferred_element_type=jnp.float32)
        .astype(jnp.bfloat16)
        .reshape(row_count, H * HD)
    )
    mid_sum = tokens_f + dot_right_t(context, w_out)
    return (
        mid_sum,
        (tokens_f, inv_rms1, gain_one, normed1, query_rot, key_rot, values, log_total, context),
        waiting,
    )


def ffn_forward(mid_sum, weight_set):
    w_gate, w_up, w_down, gain_vec = weight_set
    gain_two = gain_vec.astype(jnp.float32)
    normed_g, inv_rms2 = norm_rows(mid_sum, gain_two)
    normed2 = normed_g.astype(jnp.bfloat16)
    gate_pre = jnp.dot(normed2, w_gate, preferred_element_type=jnp.float32)
    up_proj = jnp.dot(normed2, w_up, preferred_element_type=jnp.float32)
    sigmoid_g = jax.nn.sigmoid(gate_pre)
    act_gate = gate_pre * sigmoid_g
    hidden = (act_gate * up_proj).astype(jnp.bfloat16)
    layer_out = (mid_sum + dot_right_t(hidden, w_down)).astype(
        jnp.bfloat16
    )
    return (
        layer_out,
        (inv_rms2, gain_two, normed2, gate_pre, up_proj, sigmoid_g, act_gate, hidden),
    )


def ffn_backward(cotangent, mid_sum, kept, weight_set):
    w_gate, w_up, w_down, gain_vec = weight_set
    inv_rms2, gain_two, normed2, gate_pre, up_proj, sigmoid_g, act_gate, hidden = kept
    d_hidden = jnp.dot(cotangent, w_down, preferred_element_type=jnp.float32)
    d_up = (d_hidden * act_gate).astype(jnp.bfloat16)
    d_gate = (d_hidden * up_proj * sigmoid_g * (1.0 + gate_pre * (1.0 - sigmoid_g))).astype(
        jnp.bfloat16
    )
    d_normed2 = dot_right_t(d_gate, w_gate) + dot_right_t(d_up, w_up)
    d_mid_n, term_gain = norm_back(mid_sum, inv_rms2, gain_two, d_normed2)
    d_mid = cotangent.astype(jnp.float32) + d_mid_n
    return (d_mid, (d_gate, d_up, term_gain))


def attn_backward(d_mid, kept, weight_set, total):
    w_query, w_key, w_value, w_out, gain_vec = weight_set
    tokens_f, inv_rms1, gain_one, normed1, query_rot, key_rot, values, log_total, context = kept
    row_count = tokens_f.shape[0]
    seq_count = row_count // LEN
    groups = H // KV
    cosine, sine_tab = tables(LEN, HD)
    d_mid_b = d_mid.astype(jnp.bfloat16)
    d_context = (
        jnp.dot(d_mid_b, w_out, preferred_element_type=jnp.float32)
        .astype(jnp.bfloat16)
        .reshape(seq_count, LEN, KV, groups, HD)
    )
    prob_f = jnp.exp(causal_scores(query_rot, key_rot) - log_total)
    attn_prob = prob_f.astype(jnp.bfloat16)
    d_prob = jnp.einsum("sikgd,sjkd->skgij", d_context, values, preferred_element_type=jnp.float32)
    row_delta = jnp.sum(prob_f * d_prob, axis=-1, keepdims=True)
    d_scores = (prob_f * (d_prob - row_delta) * HD ** (-0.5)).astype(jnp.bfloat16)
    d_scores, total.held = tied(d_scores, total.held)
    total.advance()
    d_key = jnp.einsum("skgij,sikgd->sjkd", d_scores, query_rot, preferred_element_type=jnp.float32)
    d_values = jnp.einsum(
        "skgij,sikgd->sjkd", attn_prob, d_context, preferred_element_type=jnp.float32
    )
    (d_scores, d_key, d_values), total.held = tied((d_scores, d_key, d_values), total.held)
    total.advance()
    d_query = jnp.einsum(
        "skgij,sjkd->sikgd", d_scores, key_rot, preferred_element_type=jnp.float32
    ).reshape(seq_count, LEN, H, HD)
    d_query_b = (
        rotate(d_query, cosine, sine_tab, -1.0).astype(jnp.bfloat16).reshape(row_count, H * HD)
    )
    d_key_b = rotate(d_key, cosine, sine_tab, -1.0).astype(jnp.bfloat16).reshape(row_count, KV * HD)
    d_values_b = d_values.astype(jnp.bfloat16).reshape(row_count, KV * HD)
    (d_query_b, d_key_b, d_values_b), total.held = tied(
        (d_query_b, d_key_b, d_values_b), total.held
    )
    total.advance()
    first = dot_left_t(normed1, jnp.concatenate([d_query_b, d_key_b], axis=1))
    second = jnp.concatenate(
        [dot_left_t(normed1, d_values_b), dot_left_t(d_mid_b, context)], axis=1
    )
    d_normed1 = (
        dot_right_t(d_query_b, w_query)
        + dot_right_t(d_key_b, w_key)
        + dot_right_t(d_values_b, w_value)
    )
    d_tok_n, term_gain = norm_back(tokens_f, inv_rms1, gain_one, d_normed1)
    grad_tokens = d_mid + d_tok_n
    return (grad_tokens, term_gain, first.astype(jnp.bfloat16), second.astype(jnp.bfloat16))


AXES = ("fsdp", "replica")


def bits_of(count):
    return count.bit_length() - 1


class Plan:
    def __init__(self, groups, copies):
        self.groups, self.copies = groups, copies
        self.group_bits, self.copy_bits = bits_of(groups), bits_of(copies)

    def swap(self, array, partner):
        pairs = []
        for group in range(self.groups):
            for copy in range(self.copies):
                to_group, to_copy = partner(group, copy)
                pairs.append((group * self.copies + copy, to_group * self.copies + to_copy))
        return lax.ppermute(array, AXES, pairs)

    def swap_group(self, array, bit):
        return self.swap(array, lambda g, r: (g ^ (1 << bit), r))

    def swap_copy(self, array, bit):
        return self.swap(array, lambda g, r: (g, r ^ (1 << bit)))

    def where(self):
        return lax.axis_index("fsdp"), lax.axis_index("replica")


def bit_at(index, bit):
    return lax.rem(lax.div(index, 1 << bit), 2)


def joined(mine, theirs, bit, axis):
    return jnp.where(
        bit == 0,
        jnp.concatenate([mine, theirs], axis=axis),
        jnp.concatenate([theirs, mine], axis=axis),
    )


def group_rows(plan, shard):
    group, copy = plan.where()
    half = shard.shape[0] // 2
    held = lax.dynamic_slice_in_dim(shard, bit_at(copy, 0) * half, half, axis=0)[None, None]
    for bit in range(plan.group_bits):
        held = joined(held, plan.swap_group(held, bit), bit_at(group, bit), 0)
    return held


def core_rows(plan, held):
    _, copy = plan.where()
    held = joined(held, plan.swap_copy(held, 0), bit_at(copy, 0), 1)
    return held.reshape(-1, held.shape[-1])


def whole_rows(plan, shard):
    return core_rows(plan, group_rows(plan, shard))


def whole_gains(plan, gains):
    group, _ = plan.where()
    held = gains
    for bit in range(plan.group_bits):
        held = joined(held, plan.swap_group(held, bit), bit_at(group, bit), 1)
    return held


def added(left, right):
    return (left.astype(jnp.float32) + right.astype(jnp.float32)).astype(jnp.bfloat16)


def pick(array, bit, axis=0):
    size = array.shape[axis] // 2
    mine = lax.dynamic_slice_in_dim(array, bit * size, size, axis=axis)
    theirs = lax.dynamic_slice_in_dim(array, (1 - bit) * size, size, axis=axis)
    return mine, theirs


def tied(pairs, held):
    return lax.optimization_barrier((pairs, held))


class Sum:
    def __init__(self, plan, mine, theirs):
        self.plan = plan
        self.count, self.rows, self.columns = mine.shape
        self.rows //= plan.groups
        self.held = added(mine, plan.swap_copy(theirs, 0))
        self.step = 0

    def advance(self):
        plan, steps, step = self.plan, self.plan.group_bits, self.step
        group, copy = plan.where()
        core = bit_at(copy, 0)
        held = self.held
        self.step += 1
        if step == 0:
            shape = (2,) * (steps + 1) + (self.rows // 2, self.columns)
            held = held.reshape((self.count,) + shape)
            held = jnp.where(core == 0, held, jnp.moveaxis(held, steps + 1, 1))
        if step <= steps:
            group_bit = [steps - 1 - step, steps - step]
            first = bit_at(group, group_bit[0]) if step < steps else bit_at(copy, 1)
            second = bit_at(group, group_bit[1]) if step > 0 else bit_at(copy, 1)

            def partner(g, r):
                order = r % 2
                if (order == 0 and step == steps) or (order == 1 and step == 0):
                    return g, r ^ 2
                return g ^ (1 << group_bit[order]), r

            mine, theirs = pick(held, jnp.where(core == 0, first, second), 1)
            self.held = added(mine, plan.swap(theirs, partner))[:, 0]
            return True
        bit = step - steps + 1
        if bit < plan.copy_bits:
            mine, theirs = pick(held, bit_at(copy, bit), self.axis(bit))
            self.held = added(mine, plan.swap_copy(theirs, bit))
            return True
        bit = 2 * plan.copy_bits - 1 - bit
        if bit > 1:
            self.held = joined(held, plan.swap_copy(held, bit), bit_at(copy, bit), self.axis(bit))
            return True
        if bit == 1:
            self.held = joined(held, plan.swap_copy(held, 1), bit_at(copy, 1), 1)
            return True
        return False

    def axis(self, bit):
        return 2 if bit == 2 else 1

    def finish(self):
        while self.advance():
            pass
        _, copy = self.plan.where()
        core = bit_at(copy, 0)
        other = self.plan.swap_copy(self.held, 0)
        return jnp.where(core == 0, self.held, other), jnp.where(core == 0, other, self.held)


def summed_gains(plan, gains):
    group, _ = plan.where()
    held = gains
    for bit in range(plan.copy_bits):
        held = held + plan.swap_copy(held, bit)
    for bit in range(plan.group_bits):
        held = held + plan.swap_group(held, bit)
    size = gains.shape[1] // plan.groups
    return lax.dynamic_slice_in_dim(held, group * size, size, axis=1)


def on_device(
    plan,
    tokens,
    attn_gain,
    w_query,
    w_key,
    w_value,
    w_out,
    ffn_gain,
    w_gate,
    w_up,
    w_down,
    cotangent,
):
    gains = whole_gains(plan, jnp.stack([attn_gain, ffn_gain]))
    qkv = whole_rows(plan, jnp.concatenate([w_query, w_key, w_value], axis=1))
    q_size, k_size = w_query.shape[1], w_key.shape[1]
    full_query, full_key, full_value = (
        qkv[:, :q_size],
        qkv[:, q_size : q_size + k_size],
        qkv[:, q_size + k_size :],
    )
    full_out = whole_rows(plan, w_out.T)
    (full_query, full_key, full_value, full_out), ffn_shards = tied(
        (full_query, full_key, full_value, full_out), (w_gate, w_up, w_down.T)
    )
    held_gate, held_up, held_down = (group_rows(plan, shard) for shard in ffn_shards)
    attn_set = (full_query, full_key, full_value, full_out, gains[0])
    mid_sum, attn_kept, held_gate = attn_forward(tokens, attn_set, held_gate)
    full_gate = core_rows(plan, held_gate)
    mid_sum, (held_up, held_down) = tied(mid_sum, (held_up, held_down))
    ffn_set = (full_gate, core_rows(plan, held_up), core_rows(plan, held_down), gains[1])
    layer_out, ffn_kept = ffn_forward(mid_sum, ffn_set)
    d_mid, ffn_parts = ffn_backward(cotangent, mid_sum, ffn_kept, ffn_set)
    d_gate, d_up, term_gain2 = ffn_parts
    normed2 = ffn_kept[2]
    hidden = ffn_kept[7]
    _, copy = plan.where()
    core = bit_at(copy, 0)
    width = hidden.shape[1] // 2

    def half_terms(index):
        def part(array):
            return lax.dynamic_slice_in_dim(array, index * width, width, axis=1)

        terms = (
            dot_left_t(normed2, part(d_gate)),
            dot_left_t(normed2, part(d_up)),
            dot_left_t(cotangent, part(hidden)),
        )
        return jnp.stack([term.astype(jnp.bfloat16) for term in terms])

    total = Sum(plan, half_terms(core), half_terms(1 - core))
    grad_tokens, term_gain1, first, second = attn_backward(d_mid, attn_kept, attn_set, total)
    mine = jnp.where(core == 0, first, second)[None]
    theirs = jnp.where(core == 0, second, first)[None]
    attn_total = Sum(plan, mine, theirs)
    gain_grads = summed_gains(plan, jnp.stack([term_gain1, term_gain2]))
    left, right = attn_total.finish()
    left, right = left[0].astype(jnp.float32), right[0].astype(jnp.float32)
    ffn_left, ffn_right = total.finish()
    ffn_grads = jnp.concatenate([ffn_left, ffn_right], axis=2).astype(jnp.float32)
    return (
        layer_out,
        grad_tokens,
        gain_grads[0],
        left[:, :q_size],
        left[:, q_size:],
        right[:, :k_size],
        right[:, k_size:].T,
        gain_grads[1],
        ffn_grads[0],
        ffn_grads[1],
        ffn_grads[2].T,
    )


def solution(mesh):
    plan = Plan(mesh.shape["fsdp"], mesh.shape["replica"])
    return jax.shard_map(
        functools.partial(on_device, plan),
        mesh=mesh,
        in_specs=(
            P(("fsdp", "replica"), None),
            P("fsdp"),
            P("fsdp", None),
            P("fsdp", None),
            P("fsdp", None),
            P(None, "fsdp"),
            P("fsdp"),
            P("fsdp", None),
            P("fsdp", None),
            P(None, "fsdp"),
            P(("fsdp", "replica"), None),
        ),
        out_specs=(
            P(("fsdp", "replica"), None),
            P(("fsdp", "replica"), None),
            P("fsdp"),
            P("fsdp", None),
            P("fsdp", None),
            P("fsdp", None),
            P(None, "fsdp"),
            P("fsdp"),
            P("fsdp", None),
            P("fsdp", None),
            P(None, "fsdp"),
        ),
        check_vma=False,
    )
```
